32 devices in a mesh: rep: 4 (over x, core), fsdp: 8 (over z, y).
Axes of the slice: x: 2, y: 2, z: 4, core: 2. Of those that a mesh axis runs over, the one named last changes fastest.
Arguments:
- normed: bfloat16 [16384, 4096], P(('rep', 'fsdp')), may hold values from -208 to 208
- cotangent: bfloat16 [16384, 2048], P(('rep', 'fsdp')), may hold values from -18 to 18
- inner_weight: float32 [4, 4096, 2048], P('rep', 'fsdp'), may hold values from -0.09865 to 0.09865
- adam_first: float32 [4, 4096, 2048], P('rep', 'fsdp'), may hold values from -0.00015258789 to 0.00015258789
- adam_second: float32 [4, 4096, 2048], P('rep', 'fsdp'), may hold values from 2.9802322e-08 to 4.7683716e-07
- anchor: float32 [4096, 2048], P('fsdp', 'rep'), may hold values from -0.09375 to 0.09375
- outer_moment: float32 [4096, 2048], P('fsdp', 'rep'), may hold values from -7.6293945e-05 to 7.6293945e-05
Outputs:
- input_grad: bfloat16 [16384, 4096], P(('rep', 'fsdp'))
- synced_weight: float32 [4096, 2048], P('fsdp')
- moment_out: float32 [4096, 2048], P('fsdp', 'rep')
The draws below stay inside these ranges and needn't reach their ends.
All inputs are finite; a program needn't handle non-finite values.
Results may differ from the reference program's by a relative error of at most 0.007.
Values may be sent and summed in bfloat16 or wider, within the bound.
No kernel may reach another device: no remote copies, remote signals or barrier semaphores. Data moves between devices by JAX's collectives and lax.ppermute only.
A program may use at most 128 MiB of HBM per device.

```python
import math
import jax
import jax.numpy as jnp
from jax import lax

D = 4096
KVW = 1024
TOK_DEV = 512
REPS = 4
TOKENS = 16384
N_FSDP = 8


def column_rise(length):
    positions = jnp.arange(length, dtype=jnp.float32)
    return jnp.sqrt(1.0 + 2.0 * positions / length)


def block_factor(key, length):
    levels = jnp.exp((jax.random.uniform(key, (32,), jnp.float32) - 0.5) * math.log(4.0))
    return jnp.repeat(levels, length // 32, total_repeat_length=length)


def draw_normed(key, part):
    scale_key, base_key = jax.random.split(key)
    block_key = jax.random.fold_in(key, 303)
    spread = jnp.exp(jax.random.uniform(scale_key, (D,), jnp.float32) * math.log(10.0)) * column_rise(D) * block_factor(block_key, D)
    base = jnp.clip(jax.random.normal(base_key, (TOKENS, D), jnp.float32), -6.0, 6.0)
    return (base * spread[None, :]).astype(jnp.bfloat16)


def draw_cotangent(key, part):
    scale_key, base_key = jax.random.split(key)
    spread = 0.3 * jnp.exp(jax.random.uniform(scale_key, (2 * KVW,), jnp.float32) * math.log(10.0))
    base = jnp.clip(jax.random.normal(base_key, (TOKENS, 2 * KVW), jnp.float32), -6.0, 6.0)
    return (base * spread[None, :]).astype(jnp.bfloat16)


def shared_anchor(key):
    base = jax.random.normal(jax.random.fold_in(key, 101), (D, 2 * KVW), jnp.float32)
    return jnp.clip(base, -6.0, 6.0) * D ** (-0.5)


def draw_anchor(key, part):
    return shared_anchor(key)


def draw_inner_weight(key, part):
    drift = jnp.clip(jax.random.normal(jax.random.fold_in(key, 202), (REPS, D, 2 * KVW), jnp.float32), -6.0, 6.0)
    apart = drift - jnp.mean(drift, axis=0, keepdims=True)
    common = jnp.clip(jax.random.normal(jax.random.fold_in(key, 204), (D, 2 * KVW), jnp.float32), -6.0, 6.0)
    return shared_anchor(key)[None, :, :] + apart * 0.0004 + common[None, :, :] * 1e-05


def level_of(stream_key, dims, shards, smallest, largest):
    def one(axis_at, blocks):
        draws = jax.random.uniform(jax.random.fold_in(jax.random.fold_in(stream_key, 6), axis_at), (blocks,), jnp.float32, smallest / len(shards), largest / len(shards))
        return jnp.repeat(jnp.exp(draws), dims[axis_at] // blocks).reshape((-1,) + (1,) * (len(dims) - axis_at - 1))

    level = one(*shards[0])
    for cut in shards[1:]:
        level = level * one(*cut)
    return level


def bell_draw(own_key, shape, scale, bound, shards=(), kind=jnp.bfloat16):
    loudness = level_of(own_key, shape, shards, -0.22, 0.18) if shards else 1.0
    entries = jax.random.normal(own_key, shape, jnp.float32) * scale * loudness
    return jnp.minimum(jnp.maximum(entries, -bound), bound).astype(kind)


def setup_inputs(seed: int = 0) -> dict:
    key_of = jax.random.split(jax.random.key(seed), 8)
    normed = draw_normed(jax.random.fold_in(key_of[7], 71), 0)
    cotangent = draw_cotangent(jax.random.fold_in(key_of[7], 71), 0)
    inner_weight = draw_inner_weight(jax.random.fold_in(key_of[7], 71), 0)
    adam_first = bell_draw(key_of[3], (REPS, D, 2 * KVW), (0.03 * (2 * D * KVW) ** -0.5), 0.00015258789, ((0, 4), (1, 8)), jnp.float32)
    adam_second = jnp.clip(jnp.exp(math.log(4.76837158203125e-07) - 2.7725887 * jax.random.uniform(key_of[4], (REPS, D, 2 * KVW), jnp.float32) ** level_of(key_of[4], (REPS, D, 2 * KVW), ((0, 4), (1, 8)), -0.2, 0.2)), 2.9802322387695312e-08, 4.76837158203125e-07)
    anchor = draw_anchor(jax.random.fold_in(key_of[7], 71), 0)
    outer_moment = bell_draw(key_of[6], (D, 2 * KVW), 0.000005, 7.62939453125e-05, ((0, 8), (1, 4)), jnp.float32)
    return dict(normed=normed, cotangent=cotangent, inner_weight=inner_weight, adam_first=adam_first, adam_second=adam_second, anchor=anchor, outer_moment=outer_moment)


BETA_ONE = 0.9
BETA_TWO = 0.95
ADAM_EPS = 1e-08
DECAY = 0.1
RATE_INNER = 0.0004
RATE_OUTER = 0.7
MOMENTUM = 0.9

def reference(normed, cotangent, inner_weight, adam_first, adam_second, anchor, outer_moment):
    width = 2 * KVW
    group_rows = TOK_DEV * N_FSDP
    inputs = normed.reshape(REPS, N_FSDP, TOK_DEV, D)
    grads_in = cotangent.reshape(REPS, N_FSDP, TOK_DEV, width)

    def one_group(members):
        x_blocks, g_blocks, weight, first, second = members

        def add_shard(accum, pair):
            x_block, g_block = pair
            partial_value = jnp.dot(x_block.astype(jnp.float32).T, g_block.astype(jnp.float32), precision=lax.Precision.HIGHEST)
            partial_value = lax.optimization_barrier(partial_value.astype(jnp.bfloat16)).astype(jnp.float32)
            return (accum + partial_value, None)
        summed, _ = lax.scan(add_shard, jnp.zeros((D, width), jnp.float32), (x_blocks, g_blocks))
        gradient = summed / group_rows
        norm_value = jnp.sqrt(jnp.sum(gradient * gradient))
        factor = jnp.minimum(1.0, 1.0 / (norm_value + 1e-06))
        clipped = gradient * factor
        first_new = BETA_ONE * first + (1.0 - BETA_ONE) * clipped
        second_new = BETA_TWO * second + (1.0 - BETA_TWO) * clipped * clipped
        updated = weight - RATE_INNER * (first_new / (jnp.sqrt(second_new) + ADAM_EPS) + DECAY * weight)
        weight_half = lax.optimization_barrier(weight.astype(jnp.bfloat16)).astype(jnp.float32)
        back = jnp.dot(g_blocks.reshape(group_rows, width).astype(jnp.float32), weight_half.T, precision=lax.Precision.HIGHEST)
        return (back.astype(jnp.bfloat16), updated)
    back, updated = lax.map(one_group, (inputs, grads_in, inner_weight, adam_first, adam_second))
    outer_step = anchor - lax.optimization_barrier(jnp.sum(updated, axis=0)) / REPS
    moment_out = MOMENTUM * outer_moment + outer_step
    synced_weight = anchor - RATE_OUTER * (outer_step + MOMENTUM * moment_out)
    return (back.reshape(TOKENS, D), synced_weight, moment_out)
```

```python
import jax
import jax.numpy as jnp
from jax import lax
from jax.sharding import PartitionSpec as P

BETA_ONE = 0.9
BETA_TWO = 0.95
ADAM_EPS = 1e-08
DECAY = 0.1
RATE_INNER = 0.0004
RATE_OUTER = 0.7
MOMENTUM = 0.9

LINE = 4
PAIR = 2
BLOCK = LINE * PAIR
CHUNKS = 2
BF16 = jnp.bfloat16
F32 = jnp.float32


def dot(a, b, dims):
    return lax.dot_general(a, b, (dims, ((), ())), preferred_element_type=F32)


def shards(normed, cotangent, inner_weight, adam_first, adam_second, anchor, outer_moment):
    weight = inner_weight[0]
    tokens, model = normed.shape
    width = cotangent.shape[1]
    n = lax.axis_size("fsdp")
    reps = lax.axis_size("rep")
    outer = n // BLOCK
    rows = model // n
    unit = rows * outer
    me = lax.axis_index("fsdp")
    z, y = (me // PAIR) % LINE, me % PAIR
    middle = (z == 1) | (z == 2)

    across = [(f, f ^ 1) for f in range(n)]

    def along(hops):
        return [
            ((a * LINE + s) * PAIR + b, (a * LINE + t) * PAIR + b)
            for a in range(outer)
            for s, t in hops
            for b in range(PAIR)
        ]

    ends = along([(0, 1), (1, 0), (2, 3), (3, 2)])
    inward = along([(0, 1), (3, 2)])
    outward = along([(1, 0), (2, 3)])
    centre = along([(1, 2), (2, 1)])
    outer_groups = [[a * BLOCK + k for a in range(outer)] for k in range(BLOCK)]

    def send(value, pairs):
        return lax.ppermute(value, "fsdp", pairs)

    def columns(zz, yy):
        parts = [
            lax.dynamic_slice(normed, (0, ((a * LINE + zz) * PAIR + yy) * rows), (tokens, rows))
            for a in range(outer)
        ]
        return parts[0] if outer == 1 else jnp.concatenate(parts, axis=1)

    chunk = width // CHUNKS

    def cut(value, c):
        return value[:, c * chunk : (c + 1) * chunk]

    far, second, near = jnp.where(z < 2, 3, 0), jnp.where(z < 2, 2, 1), z ^ 1

    cot_other = send(cotangent, across)
    x_other = {}
    for name, zz in (("far", far), ("second", second), ("near", near), ("own", z)):
        x_other[name] = send(columns(zz, 1 - y), across)

    half = weight.astype(BF16)
    if outer > 1:
        half = lax.all_gather(half, "fsdp", axis=0, tiled=True, axis_index_groups=outer_groups)
    halves = unit // CHUNKS

    def gather(piece):
        one = send(piece, ends)
        mid = send(piece, centre)
        three = send(one, centre)
        two = mid + send(mid, outward)
        three_all = three + send(three, outward)
        return one, two, three_all

    gathered = [gather(half[c * halves : (c + 1) * halves]) for c in range(CHUNKS)]
    w_near, w_second, w_far = (
        jnp.concatenate([g[k] for g in gathered], axis=0) for k in range(3)
    )

    def partial(name, zz, c):
        return dot(columns(zz, y), cut(cotangent, c), ((0,), (0,))) + dot(
            x_other[name], cut(cot_other, c), ((0,), (0,))
        )

    def reduce(c):
        first = partial("far", far, c)
        r1 = send(first.astype(BF16), inward)
        r2a = send((first + r1.astype(F32)).astype(BF16), centre)
        next_ = partial("second", second, c)
        r2b = send(next_.astype(BF16), inward)
        last = partial("near", near, c)
        r3a = send((last + r2a.astype(F32)).astype(BF16), ends)
        r3b = send((next_ + r2b.astype(F32)).astype(BF16), centre)
        own = partial("own", z, c)
        return own + r3a.astype(F32) + r3b.astype(F32)

    summed = jnp.concatenate([reduce(c) for c in range(CHUNKS)], axis=1)
    if outer > 1:
        summed = lax.psum_scatter(
            summed.astype(BF16), "fsdp", scatter_dimension=0, tiled=True,
            axis_index_groups=outer_groups,
        ).astype(F32)

    back = jnp.zeros((tokens, model), BF16)
    for zz, w in ((z, half), (near, w_near), (second, w_second), (far, w_far)):
        mine = dot(cotangent, w, ((1,), (1,))).astype(BF16)
        theirs = dot(cot_other, w, ((1,), (1,))).astype(BF16)
        came = send(theirs, across)
        for yy, value in ((y, mine), (1 - y, came)):
            for a in range(outer):
                back = lax.dynamic_update_slice(
                    back,
                    value[:, a * rows : (a + 1) * rows],
                    (0, ((a * LINE + zz) * PAIR + yy) * rows),
                )

    rep = lax.axis_index("rep")
    weight_sum = lax.psum_scatter(weight, "rep", scatter_dimension=1, tiled=True)
    step_base = anchor - (1.0 - RATE_INNER * DECAY) * weight_sum / reps
    moment_base = MOMENTUM * outer_moment + step_base
    synced_base = anchor - RATE_OUTER * (step_base + MOMENTUM * moment_base)
    synced_base = lax.all_gather(synced_base.astype(BF16), "rep", axis=1, tiled=True)

    gradient = summed / (tokens * n)
    square_sum = lax.psum(jnp.sum(gradient * gradient), "fsdp")
    factor = jnp.minimum(1.0, 1.0 / (jnp.sqrt(square_sum) + 1e-06))
    clipped = gradient * factor
    first_new = BETA_ONE * adam_first[0] + (1.0 - BETA_ONE) * clipped
    second_new = BETA_TWO * adam_second[0] + (1.0 - BETA_TWO) * clipped * clipped
    update = (first_new / (jnp.sqrt(second_new) + ADAM_EPS)).astype(BF16)

    core = rep % 2
    quarter = width // reps
    swap_core = [(r, r ^ 1) for r in range(reps)]
    swap_x = [(r, r ^ 2) for r in range(reps)]

    def pick(value, low):
        return jnp.where(
            low == 0, value[:, 0 * quarter : 1 * quarter], value[:, 1 * quarter : 2 * quarter]
        )

    def take_parity(value, which):
        return jnp.concatenate(
            [pick(value[:, : 2 * quarter], which), pick(value[:, 2 * quarter :], which)], axis=1
        )

    came = lax.ppermute(take_parity(update, 1 - core), "rep", swap_core)
    chip = (take_parity(update, core).astype(F32) + came.astype(F32)).astype(BF16)
    other = lax.ppermute(chip, "rep", swap_x)
    total = chip.astype(F32) + other.astype(F32)
    total_half = total.astype(BF16)
    total_other = lax.ppermute(total_half, "rep", swap_core)
    even = jnp.where(core == 0, total_half, total_other)
    odd = jnp.where(core == 0, total_other, total_half)
    full = jnp.concatenate(
        [even[:, :quarter], odd[:, :quarter], even[:, quarter:], odd[:, quarter:]], axis=1
    )
    scale = RATE_INNER / reps
    mine = jnp.where(rep // 2 == 0, total[:, :quarter], total[:, quarter:])
    moment_out = moment_base + scale * mine
    synced = synced_base.astype(F32) - (RATE_OUTER * (1.0 + MOMENTUM) * scale) * full.astype(F32)
    return (back, synced, moment_out)


def solution(mesh):
    placed = (
        P(("rep", "fsdp"), None),
        P(("rep", "fsdp"), None),
        P("rep", "fsdp", None),
        P("rep", "fsdp", None),
        P("rep", "fsdp", None),
        P("fsdp", "rep"),
        P("fsdp", "rep"),
    )
    return jax.shard_map(
        shards,
        mesh=mesh,
        in_specs=placed,
        out_specs=(P(("rep", "fsdp"), None), P("fsdp", None), P("fsdp", "rep")),
        check_vma=False,
    )
```

```python
import functools

import jax
import jax.numpy as jnp
from jax import lax
from jax.experimental import pallas as pl
from jax.experimental.pallas import tpu as pltpu
from jax.sharding import PartitionSpec as P

BETA_ONE = 0.9
BETA_TWO = 0.95
ADAM_EPS = 1e-08
DECAY = 0.1
RATE_INNER = 0.0004
RATE_OUTER = 0.7
MOMENTUM = 0.9

LINE = 4
PAIR = 2
BLOCK = LINE * PAIR
BF16 = jnp.bfloat16
F32 = jnp.float32


VMEM_BYTES = 40 * 1024 * 1024


def dot(a, b, dims):
    return lax.dot_general(a, b, (dims, ((), ())), preferred_element_type=F32)


def call(body, grid, prefetch, in_specs, out_specs, out_shape, scratch, aliases, flops, args):
    moved = sum(v.size * v.dtype.itemsize for v in jax.tree.leaves(out_shape))
    return pl.pallas_call(
        body,
        grid_spec=pltpu.PrefetchScalarGridSpec(
            num_scalar_prefetch=1,
            grid=grid,
            in_specs=in_specs,
            out_specs=out_specs,
            scratch_shapes=scratch,
        ),
        out_shape=out_shape,
        input_output_aliases=aliases,
        compiler_params=pltpu.CompilerParams(vmem_limit_bytes=VMEM_BYTES),
        cost_estimate=pl.CostEstimate(
            flops=flops, bytes_accessed=4 * moved, transcendentals=0
        ),
    )(prefetch, *args)


def pick_body(axis, at_ref, *refs):
    del at_ref
    out_ref, offset = refs[-1], 0
    for ref in refs[:-1]:
        size = ref.shape[axis]
        if axis:
            out_ref[:, offset : offset + size] = ref[...]
        else:
            out_ref[offset : offset + size, :] = ref[...]
        offset += size


def pick(blocks, axis):
    height = blocks[0][0].shape[0]
    sizes = [width for _, width, _ in blocks]
    shape = (height, sum(sizes)) if axis else (height * len(blocks), sizes[0])
    return call(
        functools.partial(pick_body, axis),
        (1,),
        jnp.stack([jnp.int32(i) for _, _, i in blocks]),
        [
            pl.BlockSpec((height, width), functools.partial(lambda k, j, at: (0, at[k]), k))
            for k, width in enumerate(sizes)
        ],
        pl.BlockSpec(shape, lambda j, at: (0, 0)),
        jax.ShapeDtypeStruct(shape, blocks[0][0].dtype),
        [],
        {},
        0,
        [v for v, _, _ in blocks],
    )


def product_body(chunks, added, split, at_ref, x_ref, x_other_ref, *refs):
    del at_ref
    own, other = refs[0:chunks], refs[chunks : 2 * chunks]
    came, outs = refs[2 * chunks : 2 * chunks + added], refs[2 * chunks + added :]
    for c in range(chunks):
        value = dot(x_ref[...], own[c][...], ((0,), (0,)))
        value = value + dot(x_other_ref[...], other[c][...], ((0,), (0,)))
        for ref in came:
            value = value + ref[...].astype(F32)
        if split:
            outs[c][...] = value.astype(outs[c].dtype)
        else:
            width = value.shape[1]
            outs[0][:, c * width : (c + 1) * width] = value.astype(outs[0].dtype)


def product(x, at, x_other, other_at, cot, cot_other, chunks, quarter, unit, came, dtype, split):
    tokens = x.shape[0]
    count = len(chunks)
    narrow = pl.BlockSpec((unit, quarter), lambda h, at: (0, h))
    shape = jax.ShapeDtypeStruct((unit, 2 * quarter), dtype)
    if split:
        out_specs, out_shape = [narrow] * count, [shape] * count
    else:
        out_specs = pl.BlockSpec((unit, count * quarter), lambda h, at: (0, h))
        out_shape = jax.ShapeDtypeStruct((unit, 2 * count * quarter), dtype)
    return call(
        functools.partial(product_body, count, len(came), split),
        (2,),
        jnp.stack([at, jnp.int32(other_at)]).astype(jnp.int32),
        [
            pl.BlockSpec((tokens, unit), lambda h, at: (0, at[0])),
            pl.BlockSpec((tokens, unit), lambda h, at: (0, at[1])),
            *[
                pl.BlockSpec(
                    (tokens, quarter), functools.partial(lambda c, h, at: (0, c + 2 * h), c)
                )
                for c in chunks
            ],
            *([pl.BlockSpec((tokens, quarter), lambda h, at: (0, h))] * count),
            *([narrow] * len(came)),
        ],
        out_specs,
        out_shape,
        [],
        {},
        8 * tokens * unit * quarter * count,
        (x, x_other, *([cot] * count), *(cot_other[c] for c in chunks), *came),
    )


def image_body(pieces, held, at_ref, c_ref, *refs):
    del at_ref
    others, refs = refs[:2], refs[2:]
    weights, refs = refs[:pieces], refs[pieces:]
    back_ref, theirs_ref = refs[held:]
    w = weights[0][...]
    for ref in weights[1:]:
        w = w + ref[...]
    quarter = others[0].shape[1] // 2
    back_ref[...] = dot(c_ref[...], w, ((1,), (1,))).astype(back_ref.dtype)
    value = None
    for c, ref in enumerate(others):
        for h in range(2):
            q = c + 2 * h
            term = dot(
                ref[:, h * quarter : (h + 1) * quarter],
                w[:, q * quarter : (q + 1) * quarter],
                ((1,), (1,)),
            )
            value = term if value is None else value + term
    theirs_ref[...] = value.astype(theirs_ref.dtype)


def image(back, theirs, cot, cot_other, weights, at, rows, slots, slot, model):
    tokens, width = cot.shape
    unit = weights[0].shape[0]
    step = min(rows, 256)
    each = rows // step
    wide = pl.BlockSpec((tokens, width), lambda t, at: (0, 0))
    half = pl.BlockSpec((tokens, width // 2), lambda t, at: (0, 0))
    held = [v for v in (back, theirs) if v is not None]
    base = 1 + 1 + 2 + len(weights)
    aliases = {}
    for i, v in enumerate(held):
        aliases[base + i] = 0 if v is back else 1
    return call(
        functools.partial(image_body, len(weights), len(held)),
        (unit // step,),
        at.astype(jnp.int32)[None],
        [
            wide,
            half,
            half,
            *[pl.BlockSpec((step, width), lambda t, at: (t, 0)) for _ in weights],
            *[pl.BlockSpec(memory_space=pl.ANY) for _ in held],
        ],
        [
            pl.BlockSpec(
                (tokens, step), lambda t, at: (0, (t // each * BLOCK + at[0]) * each + t % each)
            ),
            pl.BlockSpec((tokens, step), lambda t, at: (0, slot * (unit // step) + t)),
        ],
        [
            jax.ShapeDtypeStruct((tokens, model), BF16),
            jax.ShapeDtypeStruct((tokens, slots * unit), BF16),
        ],
        [],
        aliases,
        4 * tokens * unit * width,
        (cot, *cot_other, *weights, *held),
    )


def place_body(at_ref, came_ref, held_ref, back_ref):
    del at_ref, held_ref
    back_ref[...] = came_ref[...]


def place(back, came, ats, rows):
    tokens, size = came.shape
    unit = size // len(ats)
    step = rows
    each = unit // step
    return call(
        place_body,
        (size // step,),
        jnp.stack(ats).astype(jnp.int32),
        [
            pl.BlockSpec((tokens, step), lambda t, at: (0, t)),
            pl.BlockSpec(memory_space=pl.ANY),
        ],
        pl.BlockSpec((tokens, step), lambda t, at: (0, t % each * BLOCK + at[t // each])),
        jax.ShapeDtypeStruct(back.shape, back.dtype),
        [],
        {2: 0},
        0,
        (came, back),
    )


class Order:
    def __init__(self):
        self.last = None

    def tie(self, value):
        if self.last is None:
            return value
        return lax.optimization_barrier((value, self.last))[0]

    def start(self, value, pairs, axis="fsdp"):
        return lax.ppermute(self.tie(value), axis, pairs)

    def done(self, value):
        self.last = self.tie(value)
        return self.last


def shards(normed, cotangent, inner_weight, adam_first, adam_second, anchor, outer_moment):
    weight = inner_weight[0]
    tokens, model = normed.shape
    width = cotangent.shape[1]
    n = lax.axis_size("fsdp")
    reps = lax.axis_size("rep")
    outer = n // BLOCK
    rows = model // n
    me = lax.axis_index("fsdp")
    z, y = (me // PAIR) % LINE, me % PAIR
    rep = lax.axis_index("rep")
    core = rep % 2
    quarter = width // reps

    across = [(f, f ^ 1) for f in range(n)]

    def along(hops):
        return [
            ((a * LINE + s) * PAIR + b, (a * LINE + t) * PAIR + b)
            for a in range(outer)
            for s, t in hops
            for b in range(PAIR)
        ]

    ends = along([(0, 1), (1, 0), (2, 3), (3, 2)])
    inward = along([(0, 1), (3, 2)])
    outward = along([(1, 0), (2, 3)])
    centre = along([(1, 2), (2, 1)])
    outer_groups = [[a * BLOCK + k for a in range(outer)] for k in range(BLOCK)]
    swap = {k: [(r, r ^ k) for r in range(reps)] for k in range(1, reps)}

    def columns(zz, yy):
        parts = [
            lax.dynamic_slice(normed, (0, ((a * LINE + zz) * PAIR + yy) * rows), (tokens, rows))
            for a in range(outer)
        ]
        return parts[0] if outer == 1 else jnp.concatenate(parts, axis=1)

    def owned(value, r):
        return lax.dynamic_slice(value, (0, r * quarter), (value.shape[0], quarter))

    order = Order()
    start, done = order.start, order.done
    both = range(2)
    unit = rows * outer

    far, second, near = jnp.where(z < 2, 3, 0), jnp.where(z < 2, 2, 1), z ^ 1

    def column_blocks(zz, yy):
        return [(normed, rows, (a * LINE + zz) * PAIR + yy) for a in range(outer)]

    def chunk_blocks(c):
        return [(cotangent, quarter, q) for q in range(c, reps, 2)]

    state = (adam_first[0], adam_second[0], weight)

    def start_state(k, which):
        r = order.tie(rep ^ k)
        return start(pick([(state[i], quarter, r) for i in which], 0), swap[k], "rep")

    half = weight.astype(BF16)
    if outer > 1:
        half = lax.all_gather(half, "fsdp", axis=0, tiled=True, axis_index_groups=outer_groups)
    w_near = start(half, ends)
    w_mid = start(half, centre)
    cot_other = [
        start(pick(chunk_blocks(0) + column_blocks(far, 1 - y), 1), across), None
    ]
    x_at = 2 * quarter // unit
    first_one = done(start_state(1, (0,)))
    other = order.tie(1 - y)
    cot_other[1] = start(pick(chunk_blocks(1) + column_blocks(second, other), 1), across)
    moments = {2: start_state(2, (0, 1, 2))}

    def partial(zz, x_other, other_at, chunks, came=(), dtype=BF16, split=True):
        own = (normed, zz * PAIR + y) if outer == 1 else (columns(zz, y), 0 * zz)
        return product(
            *own, x_other, other_at, cotangent, cot_other, chunks, quarter, unit, came, dtype,
            split,
        )

    def plus(value, came):
        return (value.astype(F32) + came.astype(F32)).astype(BF16)

    r1, r2a, r3a, r3b = ([None, None] for _ in range(4))
    p_far, p_near = [None, None], [None, None]

    cot_other[0] = done(cot_other[0])
    (p_far[0],) = partial(far, cot_other[0], x_at, (0,))
    r1[0] = start(p_far[0], inward)
    other = order.tie(1 - y)
    x_rest = start(pick(column_blocks(near, other) + column_blocks(z, other), 1), across)
    w_near = done(w_near)
    w_across = start(w_near, centre)
    w_mid = done(w_mid)
    w_out = start(w_mid, outward)
    cot_other[1] = done(cot_other[1])
    (p_far[1],) = partial(far, cot_other[0], x_at, (1,))
    r1[1] = start(p_far[1], inward)
    p_second = partial(second, cot_other[1], x_at, (0, 1), split=False)
    r2b = start(p_second, inward)

    def images(back, theirs, weights, zz, slots, slot):
        return image(
            back, theirs, cotangent, cot_other, weights, order.tie(zz) * PAIR + y, rows,
            slots, slot, model,
        )

    r1[0] = done(r1[0])
    r2a[0] = start(plus(p_far[0], r1[0]), centre)
    back, theirs = images(None, None, (half,), z, 3, 0)
    back, theirs = images(back, theirs, (w_near,), near, 3, 1)
    moments[2] = done(moments[2])
    moments[3] = start_state(3, (0, 1, 2))
    moments[1] = start_state(1, (1, 2))
    r1[1] = done(r1[1])
    r2a[1] = start(plus(p_far[1], r1[1]), centre)
    w_across = done(w_across)
    w_last = start(w_across, outward)
    w_out = done(w_out)
    back, theirs = images(back, theirs, (w_mid, w_out), second, 3, 2)
    came_early = start(theirs, across)
    x_rest = done(x_rest)
    p_own = partial(order.tie(z), x_rest, 1, (0, 1), (), F32)
    r2a[0] = done(r2a[0])
    (p_near[0],) = partial(near, x_rest, 0, (0,), (r2a[0],))
    r3a[0] = start(p_near[0], ends)
    moments[1] = done(moments[1])
    r2b = done(r2b)

    def of_chunk(value, c):
        return [value[:, q * quarter : (q + 1) * quarter] for q in range(c, reps, 2)]

    for c in both:
        sums = [plus(v, came) for v, came in zip(of_chunk(p_second, c), of_chunk(r2b, c))]
        r3b[c] = start(jnp.concatenate(sums, axis=1), centre)
    r2a[1] = done(r2a[1])
    (p_near[1],) = partial(near, x_rest, 0, (1,), (r2a[1],))
    r3a[1] = start(p_near[1], ends)
    w_last = done(w_last)
    back, theirs = images(back, None, (w_across, w_last), far, 1, 0)
    came_late = start(theirs, across)
    moments[3] = done(moments[3])

    def pieces(value):
        return [value[i * rows : (i + 1) * rows] for i in range(value.shape[0] // rows)]

    moments = {
        1: [first_one, *pieces(moments[1])], 2: pieces(moments[2]), 3: pieces(moments[3])
    }
    came_early = done(came_early)
    other_y = [zz * PAIR + 1 - y for zz in (z, near, second)]
    back = done(place(back, came_early, other_y, rows))

    chips = range(reps // 2)
    hops = {
        2: lambda c: [(x * 2 + c, (x ^ 1) * 2 + c) for x in chips],
        3: lambda c: [(x * 2 + 1 - c, (x ^ 1) * 2 + c) for x in chips],
        1: lambda c: [(x * 2 + 1 - c, x * 2 + c) for x in chips],
    }
    squares, sent, own_gradient = [], [], []
    for c in both:
        r3a[c] = done(r3a[c])
        r3b[c] = done(r3b[c])
        total = p_own[c] + r3a[c].astype(F32) + r3b[c].astype(F32)
        if outer > 1:
            total = lax.psum_scatter(
                total.astype(BF16), "fsdp", scatter_dimension=0, tiled=True,
                axis_index_groups=outer_groups,
            ).astype(F32)
        gradient = total / (tokens * n)
        squares.append(jnp.sum(gradient * gradient))
        narrow = gradient.astype(BF16)
        here = owned(narrow, rep // 2)
        there = owned(narrow, 1 - rep // 2)
        sent.append(
            {
                2: start(there, hops[2](c), "rep"),
                3: start(there, hops[3](c), "rep"),
                1: start(here, hops[1](c), "rep"),
            }
        )
        own_gradient.append(owned(narrow, rep // 2))
        if c == 0:
            back = done(place(back, done(came_late), [far * PAIR + 1 - y], rows))

    square = jnp.broadcast_to(squares[0] + squares[1], (reps * n, 128))
    square = lax.all_to_all(order.tie(square), ("rep", "fsdp"), 0, 0, tiled=True)
    square = jnp.sum(square[:, 0].reshape(reps, n), axis=1)
    factors = jnp.minimum(1.0, 1.0 / (jnp.sqrt(square) + 1e-06))

    def update(gradient, first, second_moment, k):
        clipped = gradient.astype(F32) * lax.dynamic_index_in_dim(factors, rep ^ k, 0, False)
        first_new = BETA_ONE * first + (1.0 - BETA_ONE) * clipped
        second_new = BETA_TWO * second_moment + (1.0 - BETA_TWO) * clipped * clipped
        return first_new / (jnp.sqrt(second_new) + ADAM_EPS)

    update_sum = update(
        jnp.where(core == 0, own_gradient[0], own_gradient[1]),
        owned(adam_first[0], rep), owned(adam_second[0], rep), 0,
    )
    weight_sum = owned(weight, rep)
    for k in (1, 2, 3):
        came = [done(sent[c][k]) for c in both]
        first, second_moment, other_weight = moments[k]
        update_sum = update_sum + update(
            jnp.where(core == 0, came[0], came[1]), first, second_moment, k
        )
        weight_sum = weight_sum + other_weight
    updated_sum = (1.0 - RATE_INNER * DECAY) * weight_sum - RATE_INNER * update_sum
    outer_step = anchor - updated_sum / reps
    moment_out = MOMENTUM * outer_moment + outer_step
    synced = (anchor - RATE_OUTER * (outer_step + MOMENTUM * moment_out)).astype(BF16)

    quarters = {0: synced}
    quarters[2] = start(synced, swap[2], "rep")
    quarters[1] = start(synced, swap[1], "rep")
    quarters[1] = done(quarters[1])
    quarters[2] = done(quarters[2])
    quarters[3] = start(quarters[2], swap[1], "rep")
    whole = jnp.zeros((rows, width), F32)
    for k in (0, 1, 2, 3):
        whole = lax.dynamic_update_slice(
            whole, quarters[k].astype(F32), (0, (rep ^ k) * quarter)
        )
    return (back, whole, moment_out)


def solution(mesh):
    placed = (
        P(("rep", "fsdp"), None),
        P(("rep", "fsdp"), None),
        P("rep", "fsdp", None),
        P("rep", "fsdp", None),
        P("rep", "fsdp", None),
        P("fsdp", "rep"),
        P("fsdp", "rep"),
    )
    return jax.shard_map(
        shards,
        mesh=mesh,
        in_specs=placed,
        out_specs=(P(("rep", "fsdp"), None), P("fsdp", None), P("fsdp", "rep")),
        check_vma=False,
    )
```

```python
import functools

import jax
import jax.numpy as jnp
from jax import lax
from jax.experimental import pallas as pl
from jax.experimental.pallas import tpu as pltpu
from jax.sharding import PartitionSpec as P

BETA_ONE = 0.9
BETA_TWO = 0.95
ADAM_EPS = 1e-08
DECAY = 0.1
RATE_INNER = 0.0004
RATE_OUTER = 0.7
MOMENTUM = 0.9

LINE = 4
PAIR = 2
BLOCK = LINE * PAIR
BF16 = jnp.bfloat16
F32 = jnp.float32


VMEM_BYTES = 60 * 1024 * 1024


def dot(a, b, dims):
    return lax.dot_general(a, b, (dims, ((), ())), preferred_element_type=F32)


def call(body, grid, prefetch, in_specs, out_specs, out_shape, scratch, aliases, flops, args):
    moved = sum(v.size * v.dtype.itemsize for v in jax.tree.leaves(out_shape))
    return pl.pallas_call(
        body,
        grid_spec=pltpu.PrefetchScalarGridSpec(
            num_scalar_prefetch=1,
            grid=grid,
            in_specs=in_specs,
            out_specs=out_specs,
            scratch_shapes=scratch,
        ),
        out_shape=out_shape,
        input_output_aliases=aliases,
        compiler_params=pltpu.CompilerParams(vmem_limit_bytes=VMEM_BYTES),
        cost_estimate=pl.CostEstimate(
            flops=flops, bytes_accessed=4 * moved, transcendentals=0
        ),
    )(prefetch, *args)


def pick_body(axis, at_ref, *refs):
    del at_ref
    out_ref, offset = refs[-1], 0
    for ref in refs[:-1]:
        size = ref.shape[axis]
        if axis:
            out_ref[:, offset : offset + size] = ref[...]
        else:
            out_ref[offset : offset + size, :] = ref[...]
        offset += size


def pick(blocks, axis):
    height = blocks[0][0].shape[0]
    sizes = [width for _, width, _ in blocks]
    shape = (height, sum(sizes)) if axis else (height * len(blocks), sizes[0])
    return call(
        functools.partial(pick_body, axis),
        (1,),
        jnp.stack([jnp.int32(i) for _, _, i in blocks]),
        [
            pl.BlockSpec((height, width), functools.partial(lambda k, j, at: (0, at[k]), k))
            for k, width in enumerate(sizes)
        ],
        pl.BlockSpec(shape, lambda j, at: (0, 0)),
        jax.ShapeDtypeStruct(shape, blocks[0][0].dtype),
        [],
        {},
        0,
        [v for v, _, _ in blocks],
    )


def product_body(chunks, added, split, at_ref, x_ref, x_other_ref, *refs):
    del at_ref
    own, other = refs[0:chunks], refs[chunks : 2 * chunks]
    came, outs = refs[2 * chunks : 2 * chunks + added], refs[2 * chunks + added :]
    for c in range(chunks):
        value = dot(x_ref[...], own[c][...], ((0,), (0,)))
        value = value + dot(x_other_ref[...], other[c][...], ((0,), (0,)))
        for ref in came:
            value = value + ref[...].astype(F32)
        if split:
            outs[c][...] = value.astype(outs[c].dtype)
        else:
            width = value.shape[1]
            outs[0][:, c * width : (c + 1) * width] = value.astype(outs[0].dtype)


def product(x, at, x_other, other_at, cot, cot_other, chunks, quarter, unit, came, dtype, split):
    tokens = x.shape[0]
    count = len(chunks)
    narrow = pl.BlockSpec((unit, quarter), lambda h, at: (0, h))
    shape = jax.ShapeDtypeStruct((unit, 2 * quarter), dtype)
    if split:
        out_specs, out_shape = [narrow] * count, [shape] * count
    else:
        out_specs = pl.BlockSpec((unit, count * quarter), lambda h, at: (0, h))
        out_shape = jax.ShapeDtypeStruct((unit, 2 * count * quarter), dtype)
    return call(
        functools.partial(product_body, count, len(came), split),
        (2,),
        jnp.stack([at, jnp.int32(other_at)]).astype(jnp.int32),
        [
            pl.BlockSpec((tokens, unit), lambda h, at: (0, at[0])),
            pl.BlockSpec((tokens, unit), lambda h, at: (0, at[1])),
            *[
                pl.BlockSpec(
                    (tokens, quarter), functools.partial(lambda c, h, at: (0, c + 2 * h), c)
                )
                for c in chunks
            ],
            *([pl.BlockSpec((tokens, quarter), lambda h, at: (0, h))] * count),
            *([narrow] * len(came)),
        ],
        out_specs,
        out_shape,
        [],
        {},
        8 * tokens * unit * quarter * count,
        (x, x_other, *([cot] * count), *(cot_other[c] for c in chunks), *came),
    )


def image_body(groups, steps, held, at_ref, c_ref, *refs):
    del at_ref
    others, refs = refs[:2], refs[2:]
    weights, refs = refs[: sum(groups)], refs[sum(groups) :]
    back_ref, theirs_ref = refs[held:]
    quarter = c_ref.shape[1] // 4

    def multiply(refs):
        w = refs[0][...]
        for ref in refs[1:]:
            w = w + ref[...]
        back_ref[...] = dot(c_ref[...], w, ((1,), (1,))).astype(back_ref.dtype)
        value = None
        for c, ref in enumerate(others):
            for h in range(2):
                q = c + 2 * h
                term = dot(
                    ref[:, h * quarter : (h + 1) * quarter],
                    w[:, q * quarter : (q + 1) * quarter],
                    ((1,), (1,)),
                )
                value = term if value is None else value + term
        theirs_ref[...] = value.astype(theirs_ref.dtype)

    offset = 0
    for g, size in enumerate(groups):
        pl.when(pl.program_id(0) // steps == g)(
            functools.partial(multiply, weights[offset : offset + size])
        )
        offset += size


def image(back, cot, cot_other, groups, ats, rows, model):
    tokens, width = cot.shape
    unit = groups[0][0].shape[0]
    step = min(rows, 256)
    each = rows // step
    steps = unit // step
    half = pl.BlockSpec((tokens, width // 2), lambda t, at: (0, 0))
    held = [] if back is None else [back]
    flat = [w for group in groups for w in group]

    def weight_spec(g):
        return pl.BlockSpec(
            (step, width), lambda t, at: (jnp.clip(t - g * steps, 0, steps - 1), 0)
        )

    return call(
        functools.partial(image_body, [len(g) for g in groups], steps, len(held)),
        (len(groups) * steps,),
        jnp.stack(ats).astype(jnp.int32),
        [
            pl.BlockSpec((tokens, width), lambda t, at: (0, 0)),
            half,
            half,
            *[weight_spec(g) for g, group in enumerate(groups) for _ in group],
            *[pl.BlockSpec(memory_space=pl.ANY) for _ in held],
        ],
        [
            pl.BlockSpec(
                (tokens, step),
                lambda t, at: (
                    0, (t % steps // each * BLOCK + at[t // steps]) * each + t % each
                ),
            ),
            pl.BlockSpec((tokens, step), lambda t, at: (0, t)),
        ],
        [
            jax.ShapeDtypeStruct((tokens, model), BF16),
            jax.ShapeDtypeStruct((tokens, len(groups) * unit), BF16),
        ],
        [],
        {4 + len(flat): 0} if held else {},
        4 * tokens * unit * width * len(groups),
        (cot, *cot_other, *flat, *held),
    )


def place_body(at_ref, came_ref, held_ref, back_ref):
    del at_ref, held_ref
    back_ref[...] = came_ref[...]


def place(back, came, ats, rows):
    tokens, size = came.shape
    unit = size // len(ats)
    step = rows
    each = unit // step
    return call(
        place_body,
        (size // step,),
        jnp.stack(ats).astype(jnp.int32),
        [
            pl.BlockSpec((tokens, step), lambda t, at: (0, t)),
            pl.BlockSpec(memory_space=pl.ANY),
        ],
        pl.BlockSpec((tokens, step), lambda t, at: (0, t % each * BLOCK + at[t // each])),
        jax.ShapeDtypeStruct(back.shape, back.dtype),
        [],
        {2: 0},
        0,
        (came, back),
    )


class Order:
    def __init__(self):
        self.last = None

    def tie(self, value):
        if self.last is None:
            return value
        return lax.optimization_barrier((value, self.last))[0]

    def start(self, value, pairs, axis="fsdp"):
        self.last = self.tie(value)
        return lax.ppermute(self.last, axis, pairs)

    def done(self, value):
        self.last = self.tie(value)
        return self.last


def shards(normed, cotangent, inner_weight, adam_first, adam_second, anchor, outer_moment):
    weight = inner_weight[0]
    tokens, model = normed.shape
    width = cotangent.shape[1]
    n = lax.axis_size("fsdp")
    reps = lax.axis_size("rep")
    outer = n // BLOCK
    rows = model // n
    me = lax.axis_index("fsdp")
    z, y = (me // PAIR) % LINE, me % PAIR
    rep = lax.axis_index("rep")
    core = rep % 2
    quarter = width // reps

    across = [(f, f ^ 1) for f in range(n)]

    def along(hops):
        return [
            ((a * LINE + s) * PAIR + b, (a * LINE + t) * PAIR + b)
            for a in range(outer)
            for s, t in hops
            for b in range(PAIR)
        ]

    ends = along([(0, 1), (1, 0), (2, 3), (3, 2)])
    inward = along([(0, 1), (3, 2)])
    outward = along([(1, 0), (2, 3)])
    centre = along([(1, 2), (2, 1)])
    outer_groups = [[a * BLOCK + k for a in range(outer)] for k in range(BLOCK)]
    swap = {k: [(r, r ^ k) for r in range(reps)] for k in range(1, reps)}

    def columns(zz, yy):
        parts = [
            lax.dynamic_slice(normed, (0, ((a * LINE + zz) * PAIR + yy) * rows), (tokens, rows))
            for a in range(outer)
        ]
        return parts[0] if outer == 1 else jnp.concatenate(parts, axis=1)

    def owned(value, r):
        return lax.dynamic_slice(value, (0, r * quarter), (value.shape[0], quarter))

    order = Order()
    start, done = order.start, order.done
    both = range(2)
    unit = rows * outer

    far, second, near = jnp.where(z < 2, 3, 0), jnp.where(z < 2, 2, 1), z ^ 1

    def column_blocks(zz, yy):
        return [(normed, rows, (a * LINE + zz) * PAIR + yy) for a in range(outer)]

    def chunk_blocks(c):
        return [(cotangent, quarter, q) for q in range(c, reps, 2)]

    half = weight.astype(BF16)
    if outer > 1:
        half = lax.all_gather(half, "fsdp", axis=0, tiled=True, axis_index_groups=outer_groups)
    w_near = lax.ppermute(half, "fsdp", ends)
    w_mid = lax.ppermute(half, "fsdp", centre)
    early = pick(chunk_blocks(0) + column_blocks(far, 1 - y), 1)
    cot_other = [lax.ppermute(early, "fsdp", across), None]
    x_at = 2 * quarter // unit

    chip_at = rep // 2
    order.last = (half, early)
    mate = order.tie(1 - core)
    blocks = [(weight, quarter, 2 * x + mate) for x in range(reps // 2)]
    w_mate = done(lax.ppermute(pick(blocks, 1), "rep", swap[1]))
    other = order.tie(1 - y)
    cot_other[1] = lax.ppermute(
        pick(chunk_blocks(1) + column_blocks(second, other), 1), "fsdp", across
    )
    w_chip, w_there = (
        owned(weight, 2 * x + core) + owned(w_mate, x) for x in (chip_at, 1 - chip_at)
    )
    w_x = lax.ppermute(w_there, "rep", swap[2])

    def partial(zz, x_other, other_at, chunks, came=(), dtype=BF16, split=True):
        own = (normed, zz * PAIR + y) if outer == 1 else (columns(zz, y), 0 * zz)
        return product(
            *own, x_other, other_at, cotangent, cot_other, chunks, quarter, unit, came, dtype,
            split,
        )

    def plus(value, came):
        return (value.astype(F32) + came.astype(F32)).astype(BF16)

    r1, r2a, r3a, r3b = ([None, None] for _ in range(4))
    p_far, p_near = [None, None], [None, None]

    def images(back, groups, blocks):
        ats = [order.tie(zz) * PAIR + y for zz in blocks]
        return image(back, cotangent, cot_other, groups, ats, rows, model)

    cot_other[0] = done(cot_other[0])
    (p_far[0],) = partial(far, cot_other[0], x_at, (0,))
    r1[0] = start(p_far[0], inward)
    w_near = done(w_near)
    w_x = done(w_x)
    w_across = start(w_near, centre)
    w_mid = done(w_mid)
    w_out = start(w_mid, outward)
    other = order.tie(1 - y)
    x_rest = start(pick(column_blocks(near, other) + column_blocks(z, other), 1), across)
    cot_other[1] = done(cot_other[1])
    (p_far[1],) = partial(far, cot_other[0], x_at, (1,))
    r1[1] = start(p_far[1], inward)
    r1[0] = done(r1[0])
    r2a[0] = start(plus(p_far[0], r1[0]), centre)
    p_second = partial(order.tie(second), cot_other[1], x_at, (0, 1), split=False)
    r2b = start(p_second, inward)
    r1[1] = done(r1[1])
    r2a[1] = start(plus(p_far[1], r1[1]), centre)
    w_across = done(w_across)
    w_last = start(w_across, outward)
    w_out = done(w_out)

    back, theirs = images(
        None, ((half,), (w_near,), (w_mid, w_out)), (z, near, second)
    )
    came_early = start(theirs, across)
    x_rest = done(x_rest)
    r2a[0] = done(r2a[0])
    (p_near[0],) = partial(near, x_rest, 0, (0,), (r2a[0],))
    r3a[0] = start(p_near[0], ends)
    p_own = partial(order.tie(z), x_rest, 1, (0, 1), (), F32)
    r2b = done(r2b)

    def of_chunk(value, c):
        return [value[:, q * quarter : (q + 1) * quarter] for q in range(c, reps, 2)]

    for c in both:
        sums = [plus(v, came) for v, came in zip(of_chunk(p_second, c), of_chunk(r2b, c))]
        r3b[c] = start(jnp.concatenate(sums, axis=1), centre)
    r2a[1] = done(r2a[1])
    (p_near[1],) = partial(near, x_rest, 0, (1,), (r2a[1],))
    r3a[1] = start(p_near[1], ends)
    w_last = done(w_last)
    back, theirs = images(back, ((w_across, w_last),), (far,))
    came_late = start(theirs, across)
    came_early = done(came_early)
    other_y = [zz * PAIR + 1 - y for zz in (z, near, second)]
    back = done(place(back, came_early, other_y, rows))

    squares, gradient = [], []
    for c in both:
        r3a[c] = done(r3a[c])
        r3b[c] = done(r3b[c])
        total = p_own[c] + r3a[c].astype(F32) + r3b[c].astype(F32)
        if outer > 1:
            total = lax.psum_scatter(
                total.astype(BF16), "fsdp", scatter_dimension=0, tiled=True,
                axis_index_groups=outer_groups,
            ).astype(F32)
        gradient.append(total / (tokens * n))
        squares.append(jnp.sum(gradient[c] * gradient[c]))
        if c == 0:
            back = done(place(back, done(came_late), [far * PAIR + 1 - y], rows))

    square = jnp.broadcast_to(squares[0] + squares[1], (n, 128))
    square = lax.all_to_all(square, "fsdp", 0, 0, tiled=True)
    factor = jnp.minimum(1.0, 1.0 / (jnp.sqrt(jnp.sum(square[:, 0])) + 1e-06))

    def update(parity):
        quarters = [2 * x + parity for x in range(reps // 2)]
        first, second_moment = (
            jnp.concatenate([owned(v[0], q) for q in quarters], axis=1)
            for v in (adam_first, adam_second)
        )
        clipped = jnp.where(parity == 0, gradient[0], gradient[1]) * factor
        first_new = BETA_ONE * first + (1.0 - BETA_ONE) * clipped
        second_new = BETA_TWO * second_moment + (1.0 - BETA_TWO) * clipped * clipped
        return (first_new / (jnp.sqrt(second_new) + ADAM_EPS)).astype(BF16)

    u_mate = start(update(1 - core), swap[1], "rep")
    u_own = update(core)
    u_mate = done(u_mate)
    u_here, u_there = (
        (owned(u_own, x).astype(F32) + owned(u_mate, x).astype(F32)) for x in (chip_at, 1 - chip_at)
    )
    u_x = start(u_there.astype(BF16), swap[2], "rep")
    u_x = done(u_x)
    update_sum = u_here + u_x.astype(F32)
    weight_sum = w_chip + w_x
    updated_sum = (1.0 - RATE_INNER * DECAY) * weight_sum - RATE_INNER * update_sum
    outer_step = anchor - updated_sum / reps
    moment_out = MOMENTUM * outer_moment + outer_step
    synced = (anchor - RATE_OUTER * (outer_step + MOMENTUM * moment_out)).astype(BF16)

    quarters = {0: synced}
    quarters[2] = start(synced, swap[2], "rep")
    quarters[1] = start(synced, swap[1], "rep")
    quarters[1] = done(quarters[1])
    quarters[2] = done(quarters[2])
    quarters[3] = start(quarters[2], swap[1], "rep")
    even = {k: jnp.where(core == 0, quarters[k], quarters[k ^ 1]) for k in (0, 2)}
    odd = {k: jnp.where(core == 0, quarters[k ^ 1], quarters[k]) for k in (0, 2)}
    first_chip = rep // 2 == 0
    whole = jnp.concatenate(
        [
            jnp.where(first_chip, even[0], even[2]),
            jnp.where(first_chip, odd[0], odd[2]),
            jnp.where(first_chip, even[2], even[0]),
            jnp.where(first_chip, odd[2], odd[0]),
        ],
        axis=1,
    ).astype(F32)
    return (back, whole, moment_out)


def solution(mesh):
    placed = (
        P(("rep", "fsdp"), None),
        P(("rep", "fsdp"), None),
        P("rep", "fsdp", None),
        P("rep", "fsdp", None),
        P("rep", "fsdp", None),
        P("fsdp", "rep"),
        P("fsdp", "rep"),
    )
    return jax.shard_map(
        shards,
        mesh=mesh,
        in_specs=placed,
        out_specs=(P(("rep", "fsdp"), None), P("fsdp", None), P("fsdp", "rep")),
        check_vma=False,
    )
```

```python
import functools

import jax
import jax.numpy as jnp
from jax import lax
from jax.experimental import pallas as pl
from jax.experimental.pallas import tpu as pltpu
from jax.sharding import PartitionSpec as P

BETA_ONE = 0.9
BETA_TWO = 0.95
ADAM_EPS = 1e-08
DECAY = 0.1
RATE_INNER = 0.0004
RATE_OUTER = 0.7
MOMENTUM = 0.9

LINE = 4
PAIR = 2
BLOCK = LINE * PAIR
BF16 = jnp.bfloat16
F32 = jnp.float32


VMEM_BYTES = 60 * 1024 * 1024


def dot(a, b, dims):
    return lax.dot_general(a, b, (dims, ((), ())), preferred_element_type=F32)


def call(body, grid, prefetch, in_specs, out_specs, out_shape, scratch, aliases, flops, args):
    moved = sum(v.size * v.dtype.itemsize for v in jax.tree.leaves(out_shape))
    return pl.pallas_call(
        body,
        grid_spec=pltpu.PrefetchScalarGridSpec(
            num_scalar_prefetch=1,
            grid=grid,
            in_specs=in_specs,
            out_specs=out_specs,
            scratch_shapes=scratch,
        ),
        out_shape=out_shape,
        input_output_aliases=aliases,
        compiler_params=pltpu.CompilerParams(vmem_limit_bytes=VMEM_BYTES),
        cost_estimate=pl.CostEstimate(
            flops=flops, bytes_accessed=4 * moved, transcendentals=0
        ),
    )(prefetch, *args)


def pick_body(axis, at_ref, *refs):
    del at_ref
    out_ref, offset = refs[-1], 0
    for ref in refs[:-1]:
        size = ref.shape[axis]
        if axis:
            out_ref[:, offset : offset + size] = ref[...]
        else:
            out_ref[offset : offset + size, :] = ref[...]
        offset += size


def pick(blocks, axis):
    height = blocks[0][0].shape[0]
    sizes = [width for _, width, _ in blocks]
    shape = (height, sum(sizes)) if axis else (height * len(blocks), sizes[0])
    return call(
        functools.partial(pick_body, axis),
        (1,),
        jnp.stack([jnp.int32(i) for _, _, i in blocks]),
        [
            pl.BlockSpec((height, width), functools.partial(lambda k, j, at: (0, at[k]), k))
            for k, width in enumerate(sizes)
        ],
        pl.BlockSpec(shape, lambda j, at: (0, 0)),
        jax.ShapeDtypeStruct(shape, blocks[0][0].dtype),
        [],
        {},
        0,
        [v for v, _, _ in blocks],
    )


def front_body(picked, at_ref, weight_ref, *refs):
    del at_ref
    half_ref, early_ref, mate_ref = refs[picked + 2 :]
    half_ref[...] = weight_ref[...].astype(BF16)
    for refs, out_ref in ((refs[:picked], early_ref), (refs[picked : picked + 2], mate_ref)):
        offset = 0
        for ref in refs:
            out_ref[:, offset : offset + ref.shape[1]] = ref[...]
            offset += ref.shape[1]


def front(weight, mate, blocks, quarter):
    rows, width = weight.shape
    height = blocks[0][0].shape[0]
    steps = 4
    sizes = [size for _, size, _ in blocks] + [quarter] * 2
    ats = [jnp.int32(i) for _, _, i in blocks] + [mate, 2 + mate]
    arrays = [v for v, _, _ in blocks] + [weight] * 2
    return call(
        functools.partial(front_body, len(blocks)),
        (steps,),
        jnp.stack(ats),
        [pl.BlockSpec((rows // steps, width), lambda j, at: (j, 0))]
        + [
            pl.BlockSpec(
                (v.shape[0] // steps, size),
                functools.partial(lambda k, j, at: (j, at[k]), k),
            )
            for k, (v, size) in enumerate(zip(arrays, sizes))
        ],
        [
            pl.BlockSpec((rows // steps, width), lambda j, at: (j, 0)),
            pl.BlockSpec((height // steps, sum(sizes[:-2])), lambda j, at: (j, 0)),
            pl.BlockSpec((rows // steps, 2 * quarter), lambda j, at: (j, 0)),
        ],
        [
            jax.ShapeDtypeStruct((rows, width), BF16),
            jax.ShapeDtypeStruct((height, sum(sizes[:-2])), BF16),
            jax.ShapeDtypeStruct((rows, 2 * quarter), F32),
        ],
        [],
        {},
        0,
        (weight, *arrays),
    )


def product_body(chunks, added, split, at_ref, x_ref, x_other_ref, *refs):
    del at_ref
    own, other = refs[0:chunks], refs[chunks : 2 * chunks]
    came, outs = refs[2 * chunks : 2 * chunks + added], refs[2 * chunks + added :]
    for c in range(chunks):
        value = dot(x_ref[...], own[c][...], ((0,), (0,)))
        value = value + dot(x_other_ref[...], other[c][...], ((0,), (0,)))
        for ref in came:
            value = value + ref[...].astype(F32)
        if split:
            outs[c][...] = value.astype(outs[c].dtype)
        else:
            width = value.shape[1]
            outs[0][:, c * width : (c + 1) * width] = value.astype(outs[0].dtype)


def product(x, at, x_other, other_at, cot, cot_other, chunks, quarter, unit, came, dtype, split):
    tokens = x.shape[0]
    count = len(chunks)
    narrow = pl.BlockSpec((unit, quarter), lambda h, at: (0, h))
    shape = jax.ShapeDtypeStruct((unit, 2 * quarter), dtype)
    if split:
        out_specs, out_shape = [narrow] * count, [shape] * count
    else:
        out_specs = pl.BlockSpec((unit, count * quarter), lambda h, at: (0, h))
        out_shape = jax.ShapeDtypeStruct((unit, 2 * count * quarter), dtype)
    return call(
        functools.partial(product_body, count, len(came), split),
        (2,),
        jnp.stack([at, jnp.int32(other_at)]).astype(jnp.int32),
        [
            pl.BlockSpec((tokens, unit), lambda h, at: (0, at[0])),
            pl.BlockSpec((tokens, unit), lambda h, at: (0, at[1])),
            *[
                pl.BlockSpec(
                    (tokens, quarter), functools.partial(lambda c, h, at: (0, c + 2 * h), c)
                )
                for c in chunks
            ],
            *([pl.BlockSpec((tokens, quarter), lambda h, at: (0, h))] * count),
            *([narrow] * len(came)),
        ],
        out_specs,
        out_shape,
        [],
        {},
        8 * tokens * unit * quarter * count,
        (x, x_other, *([cot] * count), *(cot_other[c] for c in chunks), *came),
    )


def image_body(groups, steps, held, at_ref, c_ref, *refs):
    del at_ref
    others, refs = refs[:2], refs[2:]
    weights, refs = refs[: sum(groups)], refs[sum(groups) :]
    back_ref, theirs_ref = refs[held:]
    quarter = c_ref.shape[1] // 4

    def multiply(refs):
        w = refs[0][...]
        for ref in refs[1:]:
            w = w + ref[...]
        back_ref[...] = dot(c_ref[...], w, ((1,), (1,))).astype(back_ref.dtype)
        value = None
        for c, ref in enumerate(others):
            for h in range(2):
                q = c + 2 * h
                term = dot(
                    ref[:, h * quarter : (h + 1) * quarter],
                    w[:, q * quarter : (q + 1) * quarter],
                    ((1,), (1,)),
                )
                value = term if value is None else value + term
        theirs_ref[...] = value.astype(theirs_ref.dtype)

    offset = 0
    for g, size in enumerate(groups):
        pl.when(pl.program_id(0) // steps == g)(
            functools.partial(multiply, weights[offset : offset + size])
        )
        offset += size


def image(back, cot, cot_other, groups, ats, rows, model):
    tokens, width = cot.shape
    unit = groups[0][0].shape[0]
    step = min(rows, 256)
    each = rows // step
    steps = unit // step
    half = pl.BlockSpec((tokens, width // 2), lambda t, at: (0, 0))
    held = [] if back is None else [back]
    flat = [w for group in groups for w in group]

    def weight_spec(g):
        return pl.BlockSpec(
            (step, width), lambda t, at: (jnp.clip(t - g * steps, 0, steps - 1), 0)
        )

    return call(
        functools.partial(image_body, [len(g) for g in groups], steps, len(held)),
        (len(groups) * steps,),
        jnp.stack(ats).astype(jnp.int32),
        [
            pl.BlockSpec((tokens, width), lambda t, at: (0, 0)),
            half,
            half,
            *[weight_spec(g) for g, group in enumerate(groups) for _ in group],
            *[pl.BlockSpec(memory_space=pl.ANY) for _ in held],
        ],
        [
            pl.BlockSpec(
                (tokens, step),
                lambda t, at: (
                    0, (t % steps // each * BLOCK + at[t // steps]) * each + t % each
                ),
            ),
            pl.BlockSpec((tokens, step), lambda t, at: (0, t)),
        ],
        [
            jax.ShapeDtypeStruct((tokens, model), BF16),
            jax.ShapeDtypeStruct((tokens, len(groups) * unit), BF16),
        ],
        [],
        {4 + len(flat): 0} if held else {},
        4 * tokens * unit * width * len(groups),
        (cot, *cot_other, *flat, *held),
    )


def place_body(at_ref, came_ref, held_ref, back_ref):
    del at_ref, held_ref
    back_ref[...] = came_ref[...]


def place(back, came, ats, rows):
    tokens, size = came.shape
    unit = size // len(ats)
    step = rows
    each = unit // step
    return call(
        place_body,
        (size // step,),
        jnp.stack(ats).astype(jnp.int32),
        [
            pl.BlockSpec((tokens, step), lambda t, at: (0, t)),
            pl.BlockSpec(memory_space=pl.ANY),
        ],
        pl.BlockSpec((tokens, step), lambda t, at: (0, t % each * BLOCK + at[t // each])),
        jax.ShapeDtypeStruct(back.shape, back.dtype),
        [],
        {2: 0},
        0,
        (came, back),
    )


class Order:
    def __init__(self):
        self.last = None

    def tie(self, value):
        if self.last is None:
            return value
        return lax.optimization_barrier((value, self.last))[0]

    def start(self, value, pairs, axis="fsdp"):
        self.last = self.tie(value)
        return lax.ppermute(self.last, axis, pairs)

    def done(self, value):
        self.last = self.tie(value)
        return self.last


def shards(normed, cotangent, inner_weight, adam_first, adam_second, anchor, outer_moment):
    weight = inner_weight[0]
    tokens, model = normed.shape
    width = cotangent.shape[1]
    n = lax.axis_size("fsdp")
    reps = lax.axis_size("rep")
    outer = n // BLOCK
    rows = model // n
    me = lax.axis_index("fsdp")
    z, y = (me // PAIR) % LINE, me % PAIR
    rep = lax.axis_index("rep")
    core = rep % 2
    quarter = width // reps

    across = [(f, f ^ 1) for f in range(n)]

    def along(hops):
        return [
            ((a * LINE + s) * PAIR + b, (a * LINE + t) * PAIR + b)
            for a in range(outer)
            for s, t in hops
            for b in range(PAIR)
        ]

    ends = along([(0, 1), (1, 0), (2, 3), (3, 2)])
    inward = along([(0, 1), (3, 2)])
    outward = along([(1, 0), (2, 3)])
    centre = along([(1, 2), (2, 1)])
    outer_groups = [[a * BLOCK + k for a in range(outer)] for k in range(BLOCK)]
    swap = {k: [(r, r ^ k) for r in range(reps)] for k in range(1, reps)}

    def columns(zz, yy):
        parts = [
            lax.dynamic_slice(normed, (0, ((a * LINE + zz) * PAIR + yy) * rows), (tokens, rows))
            for a in range(outer)
        ]
        return parts[0] if outer == 1 else jnp.concatenate(parts, axis=1)

    def owned(value, r):
        return lax.dynamic_slice(value, (0, r * quarter), (value.shape[0], quarter))

    order = Order()
    start, done = order.start, order.done
    both = range(2)
    unit = rows * outer

    far, second, near = jnp.where(z < 2, 3, 0), jnp.where(z < 2, 2, 1), z ^ 1

    def column_blocks(zz, yy):
        return [(normed, rows, (a * LINE + zz) * PAIR + yy) for a in range(outer)]

    def chunk_blocks(c):
        return [(cotangent, quarter, q) for q in range(c, reps, 2)]

    half, early, w_mate = front(
        weight, 1 - core, chunk_blocks(0) + column_blocks(far, 1 - y), quarter
    )
    if outer > 1:
        half = lax.all_gather(half, "fsdp", axis=0, tiled=True, axis_index_groups=outer_groups)
    w_near = lax.ppermute(half, "fsdp", ends)
    w_mid = lax.ppermute(half, "fsdp", centre)
    cot_other = [lax.ppermute(early, "fsdp", across), None]
    x_at = 2 * quarter // unit

    chip_at = rep // 2
    w_mate = done(lax.ppermute(w_mate, "rep", swap[1]))
    other = order.tie(1 - y)
    cot_other[1] = lax.ppermute(
        pick(chunk_blocks(1) + column_blocks(second, other), 1), "fsdp", across
    )
    w_chip, w_there = (
        owned(weight, 2 * x + core) + owned(w_mate, x) for x in (chip_at, 1 - chip_at)
    )
    w_x = lax.ppermute(w_there, "rep", swap[2])

    def partial(zz, x_other, other_at, chunks, came=(), dtype=BF16, split=True):
        own = (normed, zz * PAIR + y) if outer == 1 else (columns(zz, y), 0 * zz)
        return product(
            *own, x_other, other_at, cotangent, cot_other, chunks, quarter, unit, came, dtype,
            split,
        )

    def plus(value, came):
        return (value.astype(F32) + came.astype(F32)).astype(BF16)

    r1, r2a, r3a, r3b = ([None, None] for _ in range(4))
    p_far, p_near = [None, None], [None, None]

    def images(back, groups, blocks):
        ats = [order.tie(zz) * PAIR + y for zz in blocks]
        return image(back, cotangent, cot_other, groups, ats, rows, model)

    cot_other[0] = done(cot_other[0])
    (p_far[0],) = partial(far, cot_other[0], x_at, (0,))
    r1[0] = start(p_far[0], inward)
    w_near = done(w_near)
    w_x = done(w_x)
    w_across = start(w_near, centre)
    w_mid = done(w_mid)
    w_out = start(w_mid, outward)
    other = order.tie(1 - y)
    x_rest = start(pick(column_blocks(near, other) + column_blocks(z, other), 1), across)
    cot_other[1] = done(cot_other[1])
    (p_far[1],) = partial(far, cot_other[0], x_at, (1,))
    r1[1] = start(p_far[1], inward)
    r1[0] = done(r1[0])
    r2a[0] = start(plus(p_far[0], r1[0]), centre)
    p_second = partial(order.tie(second), cot_other[1], x_at, (0, 1), split=False)
    r2b = start(p_second, inward)
    r1[1] = done(r1[1])
    r2a[1] = start(plus(p_far[1], r1[1]), centre)
    w_across = done(w_across)
    w_last = start(w_across, outward)
    w_out = done(w_out)

    back, theirs = images(
        None, ((half,), (w_near,), (w_mid, w_out)), (z, near, second)
    )
    came_early = start(theirs, across)
    x_rest = done(x_rest)
    r2a[0] = done(r2a[0])
    (p_near[0],) = partial(near, x_rest, 0, (0,), (r2a[0],))
    r3a[0] = start(p_near[0], ends)
    p_own = partial(order.tie(z), x_rest, 1, (0, 1), (), F32)
    r2b = done(r2b)

    def of_chunk(value, c):
        return [value[:, q * quarter : (q + 1) * quarter] for q in range(c, reps, 2)]

    for c in both:
        sums = [plus(v, came) for v, came in zip(of_chunk(p_second, c), of_chunk(r2b, c))]
        r3b[c] = start(jnp.concatenate(sums, axis=1), centre)
    r2a[1] = done(r2a[1])
    (p_near[1],) = partial(near, x_rest, 0, (1,), (r2a[1],))
    r3a[1] = start(p_near[1], ends)
    w_last = done(w_last)
    back, theirs = images(back, ((w_across, w_last),), (far,))
    came_late = start(theirs, across)
    came_early = done(came_early)
    other_y = [zz * PAIR + 1 - y for zz in (z, near, second)]
    back = done(place(back, came_early, other_y, rows))

    squares, gradient = [], []
    for c in both:
        r3a[c] = done(r3a[c])
        r3b[c] = done(r3b[c])
        total = p_own[c] + r3a[c].astype(F32) + r3b[c].astype(F32)
        if outer > 1:
            total = lax.psum_scatter(
                total.astype(BF16), "fsdp", scatter_dimension=0, tiled=True,
                axis_index_groups=outer_groups,
            ).astype(F32)
        gradient.append(total / (tokens * n))
        squares.append(jnp.sum(gradient[c] * gradient[c]))
        if c == 0:
            step_base = anchor - (1.0 - RATE_INNER * DECAY) / reps * (w_chip + w_x)
            moment_base = MOMENTUM * outer_moment + step_base
            synced_base = anchor - RATE_OUTER * (step_base + MOMENTUM * moment_base)
            synced_base = order.tie(synced_base.astype(BF16))
            synced_there = lax.ppermute(synced_base, "rep", swap[2])
            back = done(place(back, done(came_late), [far * PAIR + 1 - y], rows))

    synced_there = done(synced_there)
    square = jnp.broadcast_to(squares[0] + squares[1], (n, 128))
    square = lax.all_to_all(square, "fsdp", 0, 0, tiled=True)
    factor = jnp.minimum(1.0, 1.0 / (jnp.sqrt(jnp.sum(square[:, 0])) + 1e-06))

    def update(parity):
        quarters = [2 * x + parity for x in range(reps // 2)]
        first, second_moment = (
            jnp.concatenate([owned(v[0], q) for q in quarters], axis=1)
            for v in (adam_first, adam_second)
        )
        clipped = jnp.where(parity == 0, gradient[0], gradient[1]) * factor
        first_new = BETA_ONE * first + (1.0 - BETA_ONE) * clipped
        second_new = BETA_TWO * second_moment + (1.0 - BETA_TWO) * clipped * clipped
        return (first_new / (jnp.sqrt(second_new) + ADAM_EPS)).astype(BF16)

    u_mate, u_own = lax.optimization_barrier((update(1 - core), update(core)))
    u_mate = start(u_mate, swap[1], "rep")
    u_mate = done(u_mate)
    u_chip = (u_own.astype(F32) + u_mate.astype(F32)).astype(BF16)
    u_x = done(start(u_chip, swap[2], "rep"))
    update_sum = u_chip.astype(F32) + u_x.astype(F32)
    scale = RATE_INNER / reps
    moment_out = moment_base + scale * jnp.where(
        chip_at == 0, update_sum[:, :quarter], update_sum[:, quarter:]
    )
    base = jnp.concatenate(
        [
            jnp.where(chip_at == 0, synced_base, synced_there),
            jnp.where(chip_at == 0, synced_there, synced_base),
        ],
        axis=1,
    )
    synced = base.astype(F32) - RATE_OUTER * (1.0 + MOMENTUM) * scale * update_sum
    synced = synced.astype(BF16)
    synced_mate = done(start(synced, swap[1], "rep"))
    even = jnp.where(core == 0, synced, synced_mate)
    odd = jnp.where(core == 0, synced_mate, synced)
    whole = jnp.concatenate(
        [v[:, x * quarter : (x + 1) * quarter] for x in range(reps // 2) for v in (even, odd)],
        axis=1,
    ).astype(F32)
    return (back, whole, moment_out)


def solution(mesh):
    placed = (
        P(("rep", "fsdp"), None),
        P(("rep", "fsdp"), None),
        P("rep", "fsdp", None),
        P("rep", "fsdp", None),
        P("rep", "fsdp", None),
        P("fsdp", "rep"),
        P("fsdp", "rep"),
    )
    return jax.shard_map(
        shards,
        mesh=mesh,
        in_specs=placed,
        out_specs=(P(("rep", "fsdp"), None), P("fsdp", None), P("fsdp", "rep")),
        check_vma=False,
    )
```

```python
import functools

import jax
import jax.numpy as jnp
from jax import lax
from jax.experimental import pallas as pl
from jax.experimental.pallas import tpu as pltpu
from jax.sharding import PartitionSpec as P

BETA_ONE = 0.9
BETA_TWO = 0.95
ADAM_EPS = 1e-08
DECAY = 0.1
RATE_INNER = 0.0004
RATE_OUTER = 0.7
MOMENTUM = 0.9

LINE = 4
PAIR = 2
BLOCK = LINE * PAIR
BF16 = jnp.bfloat16
F32 = jnp.float32


VMEM_BYTES = 60 * 1024 * 1024


def dot(a, b, dims):
    return lax.dot_general(a, b, (dims, ((), ())), preferred_element_type=F32)


def call(body, grid, prefetch, in_specs, out_specs, out_shape, scratch, aliases, flops, args):
    moved = sum(v.size * v.dtype.itemsize for v in jax.tree.leaves(out_shape))
    return pl.pallas_call(
        body,
        grid_spec=pltpu.PrefetchScalarGridSpec(
            num_scalar_prefetch=1,
            grid=grid,
            in_specs=in_specs,
            out_specs=out_specs,
            scratch_shapes=scratch,
        ),
        out_shape=out_shape,
        input_output_aliases=aliases,
        compiler_params=pltpu.CompilerParams(vmem_limit_bytes=VMEM_BYTES),
        cost_estimate=pl.CostEstimate(
            flops=flops, bytes_accessed=4 * moved, transcendentals=0
        ),
    )(prefetch, *args)


def pick_body(axis, at_ref, *refs):
    del at_ref
    out_ref, offset = refs[-1], 0
    for ref in refs[:-1]:
        size = ref.shape[axis]
        if axis:
            out_ref[:, offset : offset + size] = ref[...]
        else:
            out_ref[offset : offset + size, :] = ref[...]
        offset += size


def pick(blocks, axis):
    height = blocks[0][0].shape[0]
    sizes = [width for _, width, _ in blocks]
    shape = (height, sum(sizes)) if axis else (height * len(blocks), sizes[0])
    return call(
        functools.partial(pick_body, axis),
        (1,),
        jnp.stack([jnp.int32(i) for _, _, i in blocks]),
        [
            pl.BlockSpec((height, width), functools.partial(lambda k, j, at: (0, at[k]), k))
            for k, width in enumerate(sizes)
        ],
        pl.BlockSpec(shape, lambda j, at: (0, 0)),
        jax.ShapeDtypeStruct(shape, blocks[0][0].dtype),
        [],
        {},
        0,
        [v for v, _, _ in blocks],
    )


def front_body(picked, at_ref, weight_ref, *refs):
    del at_ref
    half_ref, early_ref, mate_ref = refs[picked + 2 :]
    half_ref[...] = weight_ref[...].astype(BF16)
    for refs, out_ref in ((refs[:picked], early_ref), (refs[picked : picked + 2], mate_ref)):
        offset = 0
        for ref in refs:
            out_ref[:, offset : offset + ref.shape[1]] = ref[...]
            offset += ref.shape[1]


def front(weight, mate, blocks, quarter):
    rows, width = weight.shape
    height = blocks[0][0].shape[0]
    steps = 4
    sizes = [size for _, size, _ in blocks] + [quarter] * 2
    ats = [jnp.int32(i) for _, _, i in blocks] + [mate, 2 + mate]
    arrays = [v for v, _, _ in blocks] + [weight] * 2
    return call(
        functools.partial(front_body, len(blocks)),
        (steps,),
        jnp.stack(ats),
        [pl.BlockSpec((rows // steps, width), lambda j, at: (j, 0))]
        + [
            pl.BlockSpec(
                (v.shape[0] // steps, size),
                functools.partial(lambda k, j, at: (j, at[k]), k),
            )
            for k, (v, size) in enumerate(zip(arrays, sizes))
        ],
        [
            pl.BlockSpec((rows // steps, width), lambda j, at: (j, 0)),
            pl.BlockSpec((height // steps, sum(sizes[:-2])), lambda j, at: (j, 0)),
            pl.BlockSpec((rows // steps, 2 * quarter), lambda j, at: (j, 0)),
        ],
        [
            jax.ShapeDtypeStruct((rows, width), BF16),
            jax.ShapeDtypeStruct((height, sum(sizes[:-2])), BF16),
            jax.ShapeDtypeStruct((rows, 2 * quarter), F32),
        ],
        [],
        {},
        0,
        (weight, *arrays),
    )


def product_body(chunks, added, split, at_ref, x_ref, x_other_ref, *refs):
    del at_ref
    own, other = refs[0:chunks], refs[chunks : 2 * chunks]
    came, outs = refs[2 * chunks : 2 * chunks + added], refs[2 * chunks + added :]
    for c in range(chunks):
        value = dot(x_ref[...], own[c][...], ((0,), (0,)))
        value = value + dot(x_other_ref[...], other[c][...], ((0,), (0,)))
        for ref in came:
            value = value + ref[...].astype(F32)
        if split:
            outs[c][...] = value.astype(outs[c].dtype)
        else:
            width = value.shape[1]
            outs[0][:, c * width : (c + 1) * width] = value.astype(outs[0].dtype)


def product(x, at, x_other, other_at, cot, cot_other, chunks, quarter, unit, came, dtype, split):
    tokens = x.shape[0]
    count = len(chunks)
    narrow = pl.BlockSpec((unit, quarter), lambda h, at: (0, h))
    shape = jax.ShapeDtypeStruct((unit, 2 * quarter), dtype)
    if split:
        out_specs, out_shape = [narrow] * count, [shape] * count
    else:
        out_specs = pl.BlockSpec((unit, count * quarter), lambda h, at: (0, h))
        out_shape = jax.ShapeDtypeStruct((unit, 2 * count * quarter), dtype)
    return call(
        functools.partial(product_body, count, len(came), split),
        (2,),
        jnp.stack([at, jnp.int32(other_at)]).astype(jnp.int32),
        [
            pl.BlockSpec((tokens, unit), lambda h, at: (0, at[0])),
            pl.BlockSpec((tokens, unit), lambda h, at: (0, at[1])),
            *[
                pl.BlockSpec(
                    (tokens, quarter), functools.partial(lambda c, h, at: (0, c + 2 * h), c)
                )
                for c in chunks
            ],
            *([pl.BlockSpec((tokens, quarter), lambda h, at: (0, h))] * count),
            *([narrow] * len(came)),
        ],
        out_specs,
        out_shape,
        [],
        {},
        8 * tokens * unit * quarter * count,
        (x, x_other, *([cot] * count), *(cot_other[c] for c in chunks), *came),
    )


def image_body(groups, steps, held, at_ref, c_ref, *refs):
    del at_ref
    others, refs = refs[:2], refs[2:]
    weights, refs = refs[: sum(groups)], refs[sum(groups) :]
    back_ref, theirs_ref = refs[held:]
    quarter = c_ref.shape[1] // 4

    def multiply(refs):
        w = refs[0][...]
        for ref in refs[1:]:
            w = w + ref[...]
        back_ref[...] = dot(c_ref[...], w, ((1,), (1,))).astype(back_ref.dtype)
        value = None
        for c, ref in enumerate(others):
            for h in range(2):
                q = c + 2 * h
                term = dot(
                    ref[:, h * quarter : (h + 1) * quarter],
                    w[:, q * quarter : (q + 1) * quarter],
                    ((1,), (1,)),
                )
                value = term if value is None else value + term
        theirs_ref[...] = value.astype(theirs_ref.dtype)

    offset = 0
    for g, size in enumerate(groups):
        pl.when(pl.program_id(0) // steps == g)(
            functools.partial(multiply, weights[offset : offset + size])
        )
        offset += size


def image(back, cot, cot_other, groups, ats, rows, model):
    tokens, width = cot.shape
    unit = groups[0][0].shape[0]
    step = min(rows, 256)
    each = rows // step
    steps = unit // step
    half = pl.BlockSpec((tokens, width // 2), lambda t, at: (0, 0))
    held = [] if back is None else [back]
    flat = [w for group in groups for w in group]

    def weight_spec(g):
        return pl.BlockSpec(
            (step, width), lambda t, at: (jnp.clip(t - g * steps, 0, steps - 1), 0)
        )

    return call(
        functools.partial(image_body, [len(g) for g in groups], steps, len(held)),
        (len(groups) * steps,),
        jnp.stack(ats).astype(jnp.int32),
        [
            pl.BlockSpec((tokens, width), lambda t, at: (0, 0)),
            half,
            half,
            *[weight_spec(g) for g, group in enumerate(groups) for _ in group],
            *[pl.BlockSpec(memory_space=pl.ANY) for _ in held],
        ],
        [
            pl.BlockSpec(
                (tokens, step),
                lambda t, at: (
                    0, (t % steps // each * BLOCK + at[t // steps]) * each + t % each
                ),
            ),
            pl.BlockSpec((tokens, step), lambda t, at: (0, t)),
        ],
        [
            jax.ShapeDtypeStruct((tokens, model), BF16),
            jax.ShapeDtypeStruct((tokens, len(groups) * unit), BF16),
        ],
        [],
        {4 + len(flat): 0} if held else {},
        4 * tokens * unit * width * len(groups),
        (cot, *cot_other, *flat, *held),
    )


def place_body(at_ref, came_ref, held_ref, back_ref):
    del at_ref, held_ref
    back_ref[...] = came_ref[...]


def place(back, came, ats, rows):
    tokens, size = came.shape
    unit = size // len(ats)
    step = rows
    each = unit // step
    return call(
        place_body,
        (size // step,),
        jnp.stack(ats).astype(jnp.int32),
        [
            pl.BlockSpec((tokens, step), lambda t, at: (0, t)),
            pl.BlockSpec(memory_space=pl.ANY),
        ],
        pl.BlockSpec((tokens, step), lambda t, at: (0, t % each * BLOCK + at[t // each])),
        jax.ShapeDtypeStruct(back.shape, back.dtype),
        [],
        {2: 0},
        0,
        (came, back),
    )


class Order:
    def __init__(self):
        self.last = None

    def tie(self, value):
        if self.last is None:
            return value
        return lax.optimization_barrier((value, self.last))[0]

    def start(self, value, pairs, axis="fsdp"):
        self.last = self.tie(value)
        return lax.ppermute(self.last, axis, pairs)

    def done(self, value):
        self.last = self.tie(value)
        return self.last


def shards(normed, cotangent, inner_weight, adam_first, adam_second, anchor, outer_moment):
    weight = inner_weight[0]
    tokens, model = normed.shape
    width = cotangent.shape[1]
    n = lax.axis_size("fsdp")
    reps = lax.axis_size("rep")
    outer = n // BLOCK
    rows = model // n
    me = lax.axis_index("fsdp")
    z, y = (me // PAIR) % LINE, me % PAIR
    rep = lax.axis_index("rep")
    core = rep % 2
    quarter = width // reps

    across = [(f, f ^ 1) for f in range(n)]

    def along(hops):
        return [
            ((a * LINE + s) * PAIR + b, (a * LINE + t) * PAIR + b)
            for a in range(outer)
            for s, t in hops
            for b in range(PAIR)
        ]

    ends = along([(0, 1), (1, 0), (2, 3), (3, 2)])
    inward = along([(0, 1), (3, 2)])
    outward = along([(1, 0), (2, 3)])
    centre = along([(1, 2), (2, 1)])
    outer_groups = [[a * BLOCK + k for a in range(outer)] for k in range(BLOCK)]
    swap = {k: [(r, r ^ k) for r in range(reps)] for k in range(1, reps)}

    def columns(zz, yy):
        parts = [
            lax.dynamic_slice(normed, (0, ((a * LINE + zz) * PAIR + yy) * rows), (tokens, rows))
            for a in range(outer)
        ]
        return parts[0] if outer == 1 else jnp.concatenate(parts, axis=1)

    def owned(value, r):
        return lax.dynamic_slice(value, (0, r * quarter), (value.shape[0], quarter))

    order = Order()
    start, done = order.start, order.done
    both = range(2)
    unit = rows * outer

    far, second, near = jnp.where(z < 2, 3, 0), jnp.where(z < 2, 2, 1), z ^ 1

    def column_blocks(zz, yy):
        return [(normed, rows, (a * LINE + zz) * PAIR + yy) for a in range(outer)]

    def chunk_blocks(c):
        return [(cotangent, quarter, q) for q in range(c, reps, 2)]

    half, early, w_mate = front(
        weight, 1 - core, chunk_blocks(0) + column_blocks(far, 1 - y), quarter
    )
    if outer > 1:
        half = lax.all_gather(half, "fsdp", axis=0, tiled=True, axis_index_groups=outer_groups)
    w_near = lax.ppermute(half, "fsdp", ends)
    w_mid = lax.ppermute(half, "fsdp", centre)
    cot_other = [lax.ppermute(early, "fsdp", across), None]
    x_at = 2 * quarter // unit

    chip_at = rep // 2
    w_mate = done(lax.ppermute(w_mate, "rep", swap[1]))
    other = order.tie(1 - y)
    cot_other[1] = lax.ppermute(
        pick(chunk_blocks(1) + column_blocks(second, other), 1), "fsdp", across
    )
    w_chip, w_there = (
        owned(weight, 2 * x + core) + owned(w_mate, x) for x in (chip_at, 1 - chip_at)
    )
    w_x = lax.ppermute(w_there, "rep", swap[2])

    def partial(zz, x_other, other_at, chunks, came=(), dtype=BF16, split=True):
        own = (normed, zz * PAIR + y) if outer == 1 else (columns(zz, y), 0 * zz)
        return product(
            *own, x_other, other_at, cotangent, cot_other, chunks, quarter, unit, came, dtype,
            split,
        )

    def plus(value, came):
        return (value.astype(F32) + came.astype(F32)).astype(BF16)

    r1, r2a, r3a, r3b = ([None, None] for _ in range(4))
    p_far, p_near = [None, None], [None, None]

    def images(back, groups, blocks):
        ats = [order.tie(zz) * PAIR + y for zz in blocks]
        return image(back, cotangent, cot_other, groups, ats, rows, model)

    cot_other[0] = done(cot_other[0])
    (p_far[0],) = partial(far, cot_other[0], x_at, (0,))
    r1[0] = start(p_far[0], inward)
    w_near = done(w_near)
    w_x = done(w_x)
    w_across = start(w_near, centre)
    w_mid = done(w_mid)
    w_out = start(w_mid, outward)
    other = order.tie(1 - y)
    x_rest = start(pick(column_blocks(near, other) + column_blocks(z, other), 1), across)
    cot_other[1] = done(cot_other[1])
    (p_far[1],) = partial(far, cot_other[0], x_at, (1,))
    r1[1] = start(p_far[1], inward)
    r1[0] = done(r1[0])
    r2a[0] = start(plus(p_far[0], r1[0]), centre)
    p_second = partial(order.tie(second), cot_other[1], x_at, (0, 1), split=False)
    r2b = start(p_second, inward)
    r1[1] = done(r1[1])
    r2a[1] = start(plus(p_far[1], r1[1]), centre)
    w_across = done(w_across)
    w_last = start(w_across, outward)
    w_out = done(w_out)

    back, theirs = images(
        None, ((half,), (w_near,), (w_mid, w_out)), (z, near, second)
    )
    came_early = start(theirs, across)
    x_rest = done(x_rest)
    r2a[0] = done(r2a[0])
    (p_near[0],) = partial(near, x_rest, 0, (0,), (r2a[0],))
    r3a[0] = start(p_near[0], ends)
    p_own = partial(order.tie(z), x_rest, 1, (0, 1), (), F32)
    r2b = done(r2b)

    def of_chunk(value, c):
        return [value[:, q * quarter : (q + 1) * quarter] for q in range(c, reps, 2)]

    for c in both:
        sums = [plus(v, came) for v, came in zip(of_chunk(p_second, c), of_chunk(r2b, c))]
        r3b[c] = start(jnp.concatenate(sums, axis=1), centre)
    r2a[1] = done(r2a[1])
    (p_near[1],) = partial(near, x_rest, 0, (1,), (r2a[1],))
    r3a[1] = start(p_near[1], ends)
    w_last = done(w_last)
    back, theirs = images(back, ((w_across, w_last),), (far,))
    came_late = start(theirs, across)
    came_early = done(came_early)
    other_y = [zz * PAIR + 1 - y for zz in (z, near, second)]
    back = done(place(back, came_early, other_y, rows))

    squares, gradient = [], []
    for c in both:
        r3a[c] = done(r3a[c])
        r3b[c] = done(r3b[c])
        total = p_own[c] + r3a[c].astype(F32) + r3b[c].astype(F32)
        if outer > 1:
            total = lax.psum_scatter(
                total.astype(BF16), "fsdp", scatter_dimension=0, tiled=True,
                axis_index_groups=outer_groups,
            ).astype(F32)
        gradient.append(total / (tokens * n))
        squares.append(jnp.sum(gradient[c] * gradient[c]))
        if c == 0:
            step_base = anchor - (1.0 - RATE_INNER * DECAY) / reps * (w_chip + w_x)
            moment_base = MOMENTUM * outer_moment + step_base
            synced_base = anchor - RATE_OUTER * (step_base + MOMENTUM * moment_base)
            synced_base = order.tie(synced_base.astype(BF16))
            synced_there = lax.ppermute(synced_base, "rep", swap[2])
            back = done(place(back, done(came_late), [far * PAIR + 1 - y], rows))

    synced_there = done(synced_there)
    square = jnp.broadcast_to(squares[0] + squares[1], (n, 128))
    square = lax.all_to_all(square, "fsdp", 0, 0, tiled=True)
    factor = jnp.minimum(1.0, 1.0 / (jnp.sqrt(jnp.sum(square[:, 0])) + 1e-06))

    def update(parity, x):
        first, second_moment = (owned(v[0], 2 * x + parity) for v in (adam_first, adam_second))
        mine = [owned(g, x) for g in gradient]
        clipped = jnp.where(parity == 0, mine[0], mine[1]) * factor
        first_new = BETA_ONE * first + (1.0 - BETA_ONE) * clipped
        second_new = BETA_TWO * second_moment + (1.0 - BETA_TWO) * clipped * clipped
        return (first_new / (jnp.sqrt(second_new) + ADAM_EPS)).astype(BF16)

    u_mate, u_own = [], []
    for x in range(reps // 2):
        pair = lax.optimization_barrier((update(1 - core, x), update(core, x)))
        u_mate.append(start(pair[0], swap[1], "rep"))
        u_own.append(pair[1])
    u_chip, u_x = [], []
    for x in range(reps // 2):
        came = done(u_mate[x])
        u_chip.append((u_own[x].astype(F32) + came.astype(F32)).astype(BF16))
        u_x.append(start(u_chip[x], swap[2], "rep"))
    u_chip = jnp.concatenate(u_chip, axis=1)
    u_x = jnp.concatenate([done(v) for v in u_x], axis=1)
    update_sum = u_chip.astype(F32) + u_x.astype(F32)
    scale = RATE_INNER / reps
    moment_out = moment_base + scale * jnp.where(
        chip_at == 0, update_sum[:, :quarter], update_sum[:, quarter:]
    )
    base = jnp.concatenate(
        [
            jnp.where(chip_at == 0, synced_base, synced_there),
            jnp.where(chip_at == 0, synced_there, synced_base),
        ],
        axis=1,
    )
    synced = base.astype(F32) - RATE_OUTER * (1.0 + MOMENTUM) * scale * update_sum
    synced = synced.astype(BF16)
    synced_mate = done(start(synced, swap[1], "rep"))
    even = jnp.where(core == 0, synced, synced_mate)
    odd = jnp.where(core == 0, synced_mate, synced)
    whole = jnp.concatenate(
        [v[:, x * quarter : (x + 1) * quarter] for x in range(reps // 2) for v in (even, odd)],
        axis=1,
    ).astype(F32)
    return (back, whole, moment_out)


def solution(mesh):
    placed = (
        P(("rep", "fsdp"), None),
        P(("rep", "fsdp"), None),
        P("rep", "fsdp", None),
        P("rep", "fsdp", None),
        P("rep", "fsdp", None),
        P("fsdp", "rep"),
        P("fsdp", "rep"),
    )
    return jax.shard_map(
        shards,
        mesh=mesh,
        in_specs=placed,
        out_specs=(P(("rep", "fsdp"), None), P("fsdp", None), P("fsdp", "rep")),
        check_vma=False,
    )
```
